32 devices in a mesh: tm: 8 (over z, core), space: 2 (over x), samples: 2 (over y).
Axes of the slice: x: 2, y: 2, z: 4, core: 2. Of those that a mesh axis runs over, the one named last changes fastest.
Arguments:
- fields: bfloat16 [2, 16, 16, 128, 256], P('samples', 'tm', 'space'), may hold values from -6 to 6
- out_grad: bfloat16 [2, 16, 16, 128, 256], P('samples', 'tm', 'space'), may hold values from -6 to 6
- spatial_weight: bfloat16 [3, 3, 256, 256], replicated, may hold values from -0.125 to 0.125
- temporal_weight: bfloat16 [5, 256, 256], replicated, may hold values from -0.15625 to 0.15625
Outputs:
- block_out: bfloat16 [2, 16, 16, 128, 256], P('samples', 'tm', 'space')
- fields_grad: bfloat16 [2, 16, 16, 128, 256], P('samples', 'tm', 'space')
- spatial_grad: float32 [3, 3, 256, 256], replicated
- temporal_grad: float32 [5, 256, 256], replicated
The draws below stay inside these ranges and needn't reach their ends.
All inputs are finite; a program needn't handle non-finite values.
Results may differ from the reference program's by a relative error of at most 0.012.
Values may be sent and summed in bfloat16 or wider, within the bound.
A program may use at most 128 MiB of HBM per device.

```python
import jax
import jax.numpy as jnp

CH = 256
WIDE = 128
SAMPLES = 2
FRAMES = 16
HEIGHT = 16


def level_of(stream_key, extent, shards, least, top_value):
    def one(axis_at, shards_of):
        steps = jax.random.uniform(jax.random.fold_in(jax.random.fold_in(stream_key, 6), axis_at), (shards_of,), jnp.float32, least / len(shards), top_value / len(shards))
        return jnp.repeat(jnp.exp(steps), extent[axis_at] // shards_of).reshape((-1,) + (1,) * (len(extent) - axis_at - 1))

    factor_of = one(*shards[0])
    for cut in shards[1:]:
        factor_of = factor_of * one(*cut)
    return factor_of


def centred(own_key, shape, width, limit, split=(), dtype=jnp.bfloat16):
    result = width * jax.random.normal(own_key, shape, jnp.float32)
    if split:
        result = result * level_of(own_key, shape, split, -0.22, 0.18)
    return jnp.clip(result, -limit, limit).astype(dtype)


def setup_inputs(seed: int = 0) -> dict:
    arg_keys = jax.random.split(jax.random.key(seed), 5)
    fields = centred(arg_keys[0], (SAMPLES, FRAMES, HEIGHT, WIDE, CH), 1.0, 6.0, ((0, 2), (1, 8), (2, 2)))
    out_grad = centred(arg_keys[1], (SAMPLES, FRAMES, HEIGHT, WIDE, CH), 1.0, 6.0, ((0, 2), (1, 8), (2, 2)))
    spatial_weight = centred(arg_keys[2], (3, 3, CH, CH), (9 * CH) ** -0.5, 0.125)
    temporal_weight = centred(arg_keys[3], (5, CH, CH), (5 * CH) ** -0.5, 0.15625)
    return {"fields": fields, "out_grad": out_grad, "spatial_weight": spatial_weight, "temporal_weight": temporal_weight}


def gelu_tanh(value):
    return jax.nn.gelu(value, approximate=True)

def pad_tile(field):
    padded = jnp.pad(field, ((0, 0), (0, 0), (1, 1), (0, 0), (0, 0)), mode='wrap')
    return jnp.pad(padded, ((0, 0), (0, 0), (0, 0), (1, 1), (0, 0)))

def spatial_apply(padded, weight, offset, transpose):
    shape = padded.shape
    rows = shape[2] - 2
    cells = shape[3] - 2
    chans = shape[4]
    total = jnp.zeros((shape[0], shape[1], rows, cells, chans), jnp.float32)
    for i in range(3):
        for j in range(3):
            si = offset - i if transpose else i
            sj = offset - j if transpose else j
            piece = padded[:, :, si:si + rows, sj:sj + cells, :].reshape(-1, chans)
            tap = weight[i, j].T if transpose else weight[i, j]
            total = total + jnp.dot(piece, tap, preferred_element_type=jnp.float32).reshape(total.shape)
    return total

def reference(fields, out_grad, spatial_weight, temporal_weight):
    chans = fields.shape[4]
    nframes = fields.shape[1]
    padded = pad_tile(fields)
    hidden = spatial_apply(padded, spatial_weight, 0, False)
    act = gelu_tanh(hidden).astype(jnp.bfloat16)
    act_pad = jnp.pad(act, ((0, 0), (2, 2), (0, 0), (0, 0), (0, 0)))
    grad_pad = jnp.pad(out_grad, ((0, 0), (2, 2), (0, 0), (0, 0), (0, 0)))
    flat_grad = out_grad.reshape(-1, chans)
    block = jnp.zeros(act.shape, jnp.float32)
    act_grad = jnp.zeros(act.shape, jnp.float32)
    temporal_list = []
    for k in range(5):
        shifted = act_pad[:, k:k + nframes].reshape(-1, chans)
        block = block + jnp.dot(shifted, temporal_weight[k], preferred_element_type=jnp.float32).reshape(act.shape)
        temporal_list.append(jnp.dot(shifted.T, flat_grad, preferred_element_type=jnp.float32))
        back = grad_pad[:, 4 - k:4 - k + nframes].reshape(-1, chans)
        act_grad = act_grad + jnp.dot(back, temporal_weight[k].T, preferred_element_type=jnp.float32).reshape(act.shape)
    block_out = block.astype(jnp.bfloat16)
    act_grad = act_grad.astype(jnp.bfloat16)
    _, pullback = jax.vjp(gelu_tanh, hidden)
    hidden_grad = pullback(act_grad.astype(jnp.float32))[0].astype(jnp.bfloat16)
    rows_hg = hidden_grad.reshape(-1, chans)
    height = fields.shape[2]
    wide = fields.shape[3]
    spatial_list = []
    for i in range(3):
        for j in range(3):
            piece = padded[:, :, i:i + height, j:j + wide, :].reshape(-1, chans)
            spatial_list.append(jnp.dot(piece.T, rows_hg, preferred_element_type=jnp.float32))
    spatial_sum = jnp.stack(spatial_list).reshape(3, 3, chans, chans)
    temporal_sum = jnp.stack(temporal_list)
    grad_padded = pad_tile(hidden_grad)
    fields_grad = spatial_apply(grad_padded, spatial_weight, 2, True).astype(jnp.bfloat16)
    factor = (fields.shape[0] * nframes * height * wide) ** (-0.5)
    return (block_out, fields_grad, spatial_sum * factor, temporal_sum * factor)
```

```python
import functools

import jax
import jax.numpy as jnp
from jax import lax
from jax.experimental import pallas as pl
from jax.experimental.pallas import tpu as pltpu
from jax.sharding import PartitionSpec as P

F32 = jnp.float32
BF16 = jnp.bfloat16
MESH = pl.DeviceIdType.MESH
ROOT = 0.7978845608028654
CUBE = 0.044715
ALIGN = 16


def dot(a, b):
    return jnp.dot(a, b, preferred_element_type=F32)


def bits_of(size):
    return [b for b in range(size.bit_length()) if (1 << b) < size]


def plan(streams, orders):
    offset, steps_of = 0, []
    for (base, rows), order in zip(streams, orders):
        steps, now = [], rows
        for axis, bit in order:
            halve = now % (2 * ALIGN) == 0 and now > 4 * ALIGN + ALIGN
            size = now // 2 if halve else now
            steps.append((axis, bit, halve, size, offset))
            offset += size
            now = size
        steps_of.append(steps)
    return steps_of, offset


def kernel(
    sizes, streams, steps_of,
    x_hbm, g_hbm, w_hbm, wt_hbm,
    block_ref, fg_ref, grads_ref,
    xc, xs, xt, xhalo, gbuf, abuf, at, deriv, hgc, hgs, hghalo,
    w, wback, wt, wtback, acc, gath, sbuf, rbuf,
    lsem, hsend, hrecv, fsend, frecv, rsend, rrecv, asend, arecv,
):
    frames, height, wide, chans = xc.shape
    me, sp = lax.axis_index("tm"), lax.axis_index("space")
    here = {name: lax.axis_index(name) for name in sizes}
    has_prev, has_next = me > 0, me < sizes["tm"] - 1
    below = {"tm": lax.rem(me + sizes["tm"] - 1, sizes["tm"])}
    above = {"tm": lax.rem(me + 1, sizes["tm"])}
    left = {"space": lax.rem(sp + sizes["space"] - 1, sizes["space"])}
    right = {"space": lax.rem(sp + 1, sizes["space"])}

    def partner(axis, bit):
        at_bit = lax.rem(here[axis] // (1 << bit), 2)
        return {axis: here[axis] + (1 - 2 * at_bit) * (1 << bit)}, at_bit

    local = [
        pltpu.make_async_copy(src, dst, lsem.at[n])
        for n, (src, dst) in enumerate(
            ((x_hbm, xc), (w_hbm, w), (wt_hbm, wt), (g_hbm, gbuf.at[pl.ds(2, frames)]))
        )
    ]
    for copy in local:
        copy.start()

    barrier = pltpu.get_barrier_semaphore()
    peers = [left, right] + [partner(a, b)[0] for a in sizes for b in bits_of(sizes[a])]
    for peer in peers:
        pl.semaphore_signal(barrier, inc=1, device_id=peer, device_id_type=MESH)

    @pl.when(has_prev)
    def _():
        pl.semaphore_signal(barrier, inc=1, device_id=below, device_id_type=MESH)

    @pl.when(has_next)
    def _():
        pl.semaphore_signal(barrier, inc=1, device_id=above, device_id_type=MESH)

    pl.semaphore_wait(
        barrier, len(peers) + jnp.minimum(me, 1) + jnp.minimum(sizes["tm"] - 1 - me, 1)
    )

    def remote(src, dst, send, recv, peer):
        return pltpu.make_async_remote_copy(
            src_ref=src, dst_ref=dst, send_sem=send, recv_sem=recv,
            device_id=peer, device_id_type=MESH,
        )

    def row_pair(src, halo, send, recv, first):
        return [
            remote(src.at[:, height - 1], halo.at[0], send.at[first], recv.at[first], right),
            remote(src.at[:, 0], halo.at[1], send.at[first + 1], recv.at[first + 1], left),
        ]

    def frame_pair(src, start, buf, first):
        return (
            remote(
                src.at[pl.ds(start + frames - 2, 2)], buf.at[pl.ds(0, 2)],
                fsend.at[first], frecv.at[first], above,
            ),
            remote(
                src.at[pl.ds(start, 2)], buf.at[pl.ds(2 + frames, 2)],
                fsend.at[first + 1], frecv.at[first + 1], below,
            ),
        )

    def frames_start(pair):
        @pl.when(has_next)
        def _():
            pair[0].start()

        @pl.when(has_prev)
        def _():
            pair[1].start()

    def frames_wait(pair):
        @pl.when(has_next)
        def _():
            pair[0].wait_send()
            pair[1].wait_recv()

        @pl.when(has_prev)
        def _():
            pair[1].wait_send()
            pair[0].wait_recv()

    x_rows = row_pair(x_hbm, xhalo, hsend, hrecv, 0)
    g_frames = frame_pair(g_hbm, 0, gbuf, 0)
    frames_start(g_frames)
    for copy in x_rows:
        copy.start()

    for buf in (gbuf, abuf):
        @pl.when(jnp.logical_not(has_prev))
        def _(buf=buf):
            buf[0:2] = jnp.zeros((2, height, wide, chans), BF16)

        @pl.when(jnp.logical_not(has_next))
        def _(buf=buf):
            buf[2 + frames :] = jnp.zeros((2, height, wide, chans), BF16)

    cell = lax.broadcasted_iota(jnp.int32, (wide, chans), 0)

    def spread(value, dst, f, r):
        full = value.astype(F32)
        lo = jnp.where(cell == 0, 0.0, pltpu.roll(full, 1, 0)).astype(BF16)
        hi = jnp.where(cell == wide - 1, 0.0, pltpu.roll(full, wide - 1, 0)).astype(BF16)
        dst[f, r, :, 0:chans] = lo
        dst[f, r, :, chans : 2 * chans] = value
        dst[f, r, :, 2 * chans : 3 * chans] = hi

    local[0].wait()

    @pl.loop(0, frames * height)
    def _(n):
        f, r = n // height, lax.rem(n, height)
        value = xc[f, r]
        spread(value, xs, f, r + 1)
        xt[f, r + 1] = value.T

    local[1].wait()

    def settle(hidden, f, r, rows):
        square = hidden * hidden
        t = jnp.tanh(ROOT * hidden * (1.0 + CUBE * square))
        half = 0.5 * (1.0 + t)
        act = (hidden * half).astype(BF16)
        slope = half + (0.5 * ROOT) * hidden * (1.0 - t * t) * (1.0 + (3.0 * CUBE) * square)
        deriv[f, pl.ds(r, rows)] = slope.reshape(rows, wide, chans)
        abuf[2 + f, pl.ds(r, rows)] = act.reshape(rows, wide, chans)
        for n in range(rows):
            at[f, r + n] = act[n * wide : (n + 1) * wide].T

    def taps(src, f, r, rows):
        return jnp.concatenate(
            [src[f, pl.ds(r + i, rows)].reshape(rows * wide, 3 * chans) for i in range(3)], axis=1
        )

    @pl.loop(0, frames)
    def _(f):
        settle(dot(taps(xs, f, 1, height - 2), w[...]), f, 1, height - 2)

    for n in range(9):
        wback[(8 - n) * chans : (9 - n) * chans] = w[n * chans : (n + 1) * chans].T
    local[2].wait()
    for n in range(5):
        wtback[(4 - n) * chans : (5 - n) * chans] = wt[n * chans : (n + 1) * chans].T

    for copy in x_rows:
        copy.wait()

    @pl.loop(0, frames)
    def _(f):
        for side in range(2):
            value = xhalo[side, f]
            spread(value, xs, f, side * (height + 1))
            xt[f, side * (height + 1)] = value.T

    @pl.loop(0, frames)
    def _(f):
        lhs = jnp.concatenate([taps(xs, f, 0, 1), taps(xs, f, height - 1, 1)], axis=0)
        hidden = dot(lhs, w[...])
        settle(hidden[:wide], f, 0, 1)
        settle(hidden[wide:], f, height - 1, 1)

    a_frames = frame_pair(abuf, 2, abuf, 2)
    frames_start(a_frames)

    local[3].wait()
    frames_wait(g_frames)

    def over_frames(buf, f, weight):
        lhs = jnp.concatenate(
            [buf[f + k].reshape(height * wide, chans) for k in range(5)], axis=1
        )
        return dot(lhs, weight[...])

    @pl.loop(0, frames)
    def _(f):
        act_grad = over_frames(gbuf, f, wtback).astype(BF16).astype(F32)
        hg = act_grad * deriv[f].reshape(height * wide, chans)
        hgc[f] = hg.astype(BF16).reshape(height, wide, chans)

    h_rows = row_pair(hgc, hghalo, hsend, hrecv, 2)
    for copy in h_rows:
        copy.start()

    def exchange(stream, k):
        axis, bit, halve, size, offset = steps_of[stream][k]
        peer, at_bit = partner(axis, bit)
        start = segment(stream, k)
        source = start + (1 - at_bit) * size if halve else start
        copy = remote(
            sbuf.at[pl.ds(offset, size)], rbuf.at[pl.ds(offset, size)],
            rsend.at[stream, k], rrecv.at[stream, k], peer,
        )
        return copy, pl.multiple_of(source, ALIGN), size, offset

    def segment(stream, k):
        start = streams[stream][0]
        for axis, bit, halve, size, _ in steps_of[stream][:k]:
            if halve:
                start = start + partner(axis, bit)[1] * size
        return pl.multiple_of(start, ALIGN) if k else start

    def reduce_start(stream, k):
        copy, source, size, offset = exchange(stream, k)
        sbuf[offset : offset + size] = acc[pl.ds(source, size)].astype(BF16)
        copy.start()

    def reduce_finish(stream, k):
        copy, _, size, offset = exchange(stream, k)
        copy.wait()
        halve = steps_of[stream][k][2]
        keep = segment(stream, k + 1)
        got = rbuf[offset : offset + size].astype(F32)
        if halve:
            mine = acc[pl.ds(keep, size)]
        else:
            mine = sbuf[offset : offset + size].astype(F32)
        acc[pl.ds(keep, size)] = mine + got

    def round_sum(stream):
        size = steps_of[stream][-1][3]
        place = segment(stream, len(steps_of[stream]))
        gath[pl.ds(place, size)] = acc[pl.ds(place, size)].astype(BF16)

    def gather_copy(stream, k):
        axis, bit, _, size, _ = steps_of[stream][k]
        place = gath.at[pl.ds(segment(stream, k + 1), size)]
        return remote(
            place, place, asend.at[stream, k], arecv.at[stream, k], partner(axis, bit)[0]
        )

    def states(stream):
        count = len(steps_of[stream])
        halving = [k for k in range(count) if steps_of[stream][k][2]][::-1]
        moves = [lambda: reduce_start(stream, 0)]
        for k in range(1, count):
            def move(k=k):
                reduce_finish(stream, k - 1)
                reduce_start(stream, k)
            moves.append(move)

        def turn():
            reduce_finish(stream, count - 1)
            round_sum(stream)
            gather_copy(stream, halving[0]).start()

        moves.append(turn)
        for last, now in zip(halving, halving[1:]):
            def move(last=last, now=now):
                gather_copy(stream, last).wait()
                gather_copy(stream, now).start()
            moves.append(move)
        moves.append(lambda: gather_copy(stream, halving[-1]).wait())
        return moves

    queues = [states(s) for s in range(len(streams))]

    def advance(*which):
        for s in which:
            if queues[s]:
                queues[s].pop(0)()

    turned = jnp.concatenate(
        [at[f, r] for f in range(frames) for r in range(height)], axis=1
    )
    for k in range(5):
        rhs = gbuf[4 - k : 4 - k + frames].reshape(frames * height * wide, chans)
        acc[k * chans : (k + 1) * chans] = dot(turned, rhs)
    advance(0)

    @pl.loop(0, frames * height)
    def _(n):
        f, r = n // height, lax.rem(n, height)
        spread(hgc[f, r], hgs, f, r + 1)

    for i in range(3):
        lhs = jnp.concatenate(
            [xt[f, r + i] for f in range(frames) for r in range(height)], axis=1
        )
        rhs = hgs[:, 1 : height + 1].reshape(frames * height * wide, 3 * chans)
        out = dot(lhs, rhs)
        for j in range(3):
            first = (5 + 3 * i + j) * chans
            acc[first : first + chans] = out[:, (2 - j) * chans : (3 - j) * chans]
        if i == 0:
            advance(0)
        if i == 1:
            advance(1)
    advance(2, 0)

    for copy in h_rows:
        copy.wait()

    @pl.loop(0, frames)
    def _(f):
        for side in range(2):
            spread(hghalo[side, f], hgs, f, side * (height + 1))

    advance(1, 2, 0)
    for f in range(frames):
        fg_ref[f] = (
            dot(taps(hgs, f, 0, height), wback[...]).astype(BF16).reshape(height, wide, chans)
        )
        advance(1, 2, 0)

    frames_wait(a_frames)
    for f in range(frames):
        block_ref[f] = over_frames(abuf, f, wt).astype(BF16).reshape(height, wide, chans)
        advance(1, 2, 0)
    while any(queues):
        advance(1, 2, 0)
    grads_ref[...] = gath[...]


def shards(sizes, fields, out_grad, spatial_weight, temporal_weight):
    samples, frames, height, wide, chans = fields.shape
    ntaps, ktaps = 9, temporal_weight.shape[0]
    streams = [
        (0, ktaps * chans),
        (ktaps * chans, 5 * chans),
        ((ktaps + 5) * chans, 4 * chans),
    ]
    core = [("tm", 0)]
    chips = [("tm", b) for b in bits_of(sizes["tm"])[1:]]
    space = [("space", b) for b in bits_of(sizes["space"])]
    samp = [("samples", b) for b in bits_of(sizes["samples"])]
    orders = [
        core + samp + space + chips,
        core + space + samp + chips,
        core + samp + space + chips,
    ]
    steps_of, buffer_rows = plan(streams, orders)
    most = max(len(steps) for steps in steps_of)
    rows_all = (ntaps + ktaps) * chans
    tile = (height, wide, chans)
    sem = pltpu.SemaphoreType.DMA
    any_spec = pl.BlockSpec(memory_space=pl.ANY)
    vmem_spec = pl.BlockSpec(memory_space=pltpu.VMEM)
    block, fg, grads = pl.pallas_call(
        functools.partial(kernel, sizes, streams, steps_of),
        out_shape=(
            jax.ShapeDtypeStruct((samples * frames,) + tile, BF16),
            jax.ShapeDtypeStruct((samples * frames,) + tile, BF16),
            jax.ShapeDtypeStruct((rows_all, chans), BF16),
        ),
        in_specs=[any_spec] * 4,
        out_specs=(vmem_spec, vmem_spec, vmem_spec),
        scratch_shapes=[
            pltpu.VMEM((frames,) + tile, BF16),
            pltpu.VMEM((frames, height + 2, wide, 3 * chans), BF16),
            pltpu.VMEM((frames, height + 2, chans, wide), BF16),
            pltpu.VMEM((2, frames, wide, chans), BF16),
            pltpu.VMEM((frames + 4,) + tile, BF16),
            pltpu.VMEM((frames + 4,) + tile, BF16),
            pltpu.VMEM((frames, height, chans, wide), BF16),
            pltpu.VMEM((frames,) + tile, F32),
            pltpu.VMEM((frames,) + tile, BF16),
            pltpu.VMEM((frames, height + 2, wide, 3 * chans), BF16),
            pltpu.VMEM((2, frames, wide, chans), BF16),
            pltpu.VMEM((ntaps * chans, chans), BF16),
            pltpu.VMEM((ntaps * chans, chans), BF16),
            pltpu.VMEM((ktaps * chans, chans), BF16),
            pltpu.VMEM((ktaps * chans, chans), BF16),
            pltpu.VMEM((rows_all, chans), F32),
            pltpu.VMEM((rows_all, chans), BF16),
            pltpu.VMEM((buffer_rows, chans), BF16),
            pltpu.VMEM((buffer_rows, chans), BF16),
            sem((4,)), sem((4,)), sem((4,)), sem((4,)), sem((4,)),
            sem((3, most)), sem((3, most)), sem((3, most)), sem((3, most)),
        ],
        compiler_params=pltpu.CompilerParams(
            collective_id=0, has_side_effects=True, vmem_limit_bytes=60 * 1024 * 1024
        ),
    )(
        fields.reshape((samples * frames,) + tile),
        out_grad.reshape((samples * frames,) + tile),
        spatial_weight.reshape(ntaps * chans, chans),
        temporal_weight.reshape(ktaps * chans, chans),
    )
    devices = sizes["tm"] * sizes["space"] * sizes["samples"]
    factor = (samples * frames * height * wide * devices) ** (-0.5)
    scaled = grads.astype(F32) * factor
    return (
        block.reshape(fields.shape),
        fg.reshape(fields.shape),
        scaled[ktaps * chans :].reshape(spatial_weight.shape),
        scaled[: ktaps * chans].reshape(temporal_weight.shape),
    )


def solution(mesh):
    split = P("samples", "tm", "space", None, None)
    return jax.shard_map(
        functools.partial(shards, dict(mesh.shape)),
        mesh=mesh,
        in_specs=(split, split, P(), P()),
        out_specs=(split, split, P(), P()),
        check_vma=False,
    )
```

```python
import functools

import jax
import jax.numpy as jnp
from jax import lax
from jax.experimental import pallas as pl
from jax.experimental.pallas import tpu as pltpu
from jax.sharding import PartitionSpec as P

F32 = jnp.float32
BF16 = jnp.bfloat16
MESH = pl.DeviceIdType.MESH
ROOT = 0.7978845608028654
CUBE = 0.044715
ALIGN = 16


def dot(a, b):
    return jnp.dot(a, b, preferred_element_type=F32)


def bits_of(size):
    return [b for b in range(size.bit_length()) if (1 << b) < size]


def plan(streams, orders, group):
    offset, steps_of = 0, []
    for (_, rows), order in zip(streams, orders):
        steps, now = [], rows
        for axis, bit in order:
            halve = now % (2 * ALIGN) == 0
            now = now // 2 if halve else now
            steps.append(("halve" if halve else "whole", axis, bit, now, offset))
            offset += now
        axis, shift, size = group
        if size > 1 and now % (size * ALIGN) == 0:
            now //= size
            steps.append(("group", axis, shift, now, offset))
            offset += now * (size - 1)
        elif size > 1:
            for bit in bits_of(size):
                steps.append(("whole", axis, bit + shift, now, offset))
                offset += now
        steps_of.append(steps)
    return steps_of, offset


def kernel(
    sizes, streams, steps_of, chips,
    x_hbm, g_hbm, w_hbm, wt_hbm,
    block_ref, fg_ref, sgrad_ref, tgrad_ref,
    xc, xs, xt, xhalo, gbuf, abuf, at, deriv, hgc, hgs, hghalo,
    w, wback, wt, wtback, acc, gath, sbuf, rbuf,
    stage, lsem, osem, hsend, hrecv, fsend, frecv, rsend, rrecv, asend, arecv,
):
    frames, height, wide, chans = xc.shape
    me, sp = lax.axis_index("tm"), lax.axis_index("space")
    here = {name: lax.axis_index(name) for name in sizes}
    has_prev, has_next = me > 0, me < sizes["tm"] - 1
    below = {"tm": lax.rem(me + sizes["tm"] - 1, sizes["tm"])}
    above = {"tm": lax.rem(me + 1, sizes["tm"])}
    left = {"space": lax.rem(sp + sizes["space"] - 1, sizes["space"])}
    right = {"space": lax.rem(sp + 1, sizes["space"])}

    def partner(axis, bit):
        at_bit = lax.rem(here[axis] // (1 << bit), 2)
        return {axis: here[axis] + (1 - 2 * at_bit) * (1 << bit)}, at_bit

    local = [
        pltpu.make_async_copy(src, dst, lsem.at[n])
        for n, (src, dst) in enumerate(
            ((x_hbm, xc), (w_hbm, w), (wt_hbm, wt), (g_hbm, gbuf.at[pl.ds(2, frames)]))
        )
    ]
    for copy in local:
        copy.start()

    chip, core = here["tm"] // 2, lax.rem(here["tm"], 2)

    def chip_peer(step):
        return {"tm": lax.rem(chip + step + chips, chips) * 2 + core}

    barrier = pltpu.get_barrier_semaphore()
    peers = [left, right, partner("tm", 0)[0]] + [chip_peer(d) for d in range(1, chips)]
    peers += [partner(a, b)[0] for a in ("space", "samples") for b in bits_of(sizes[a])]
    for peer in peers:
        pl.semaphore_signal(barrier, inc=1, device_id=peer, device_id_type=MESH)

    @pl.when(has_prev)
    def _():
        pl.semaphore_signal(barrier, inc=1, device_id=below, device_id_type=MESH)

    @pl.when(has_next)
    def _():
        pl.semaphore_signal(barrier, inc=1, device_id=above, device_id_type=MESH)

    pl.semaphore_wait(
        barrier, len(peers) + jnp.minimum(me, 1) + jnp.minimum(sizes["tm"] - 1 - me, 1)
    )

    def remote(src, dst, send, recv, peer):
        return pltpu.make_async_remote_copy(
            src_ref=src, dst_ref=dst, send_sem=send, recv_sem=recv,
            device_id=peer, device_id_type=MESH,
        )

    def row_pair(src, halo, send, recv, first):
        return [
            remote(src.at[:, height - 1], halo.at[0], send.at[first], recv.at[first], right),
            remote(src.at[:, 0], halo.at[1], send.at[first + 1], recv.at[first + 1], left),
        ]

    def frame_pair(src, start, buf, first):
        return (
            remote(
                src.at[pl.ds(start + frames - 2, 2)], buf.at[pl.ds(0, 2)],
                fsend.at[first], frecv.at[first], above,
            ),
            remote(
                src.at[pl.ds(start, 2)], buf.at[pl.ds(2 + frames, 2)],
                fsend.at[first + 1], frecv.at[first + 1], below,
            ),
        )

    def frames_start(pair):
        @pl.when(has_next)
        def _():
            pair[0].start()

        @pl.when(has_prev)
        def _():
            pair[1].start()

    def frames_wait(pair):
        @pl.when(has_next)
        def _():
            pair[0].wait_send()
            pair[1].wait_recv()

        @pl.when(has_prev)
        def _():
            pair[1].wait_send()
            pair[0].wait_recv()

    x_rows = row_pair(x_hbm, xhalo, hsend, hrecv, 0)
    g_frames = frame_pair(g_hbm, 0, gbuf, 0)
    frames_start(g_frames)
    for copy in x_rows:
        copy.start()

    for buf in (gbuf, abuf):
        @pl.when(jnp.logical_not(has_prev))
        def _(buf=buf):
            buf[0:2] = jnp.zeros((2, height, wide, chans), BF16)

        @pl.when(jnp.logical_not(has_next))
        def _(buf=buf):
            buf[2 + frames :] = jnp.zeros((2, height, wide, chans), BF16)

    cell = lax.broadcasted_iota(jnp.int32, (wide, chans), 0)

    def spread(value, dst, f, r):
        full = value.astype(F32)
        lo = jnp.where(cell == 0, 0.0, pltpu.roll(full, 1, 0)).astype(BF16)
        hi = jnp.where(cell == wide - 1, 0.0, pltpu.roll(full, wide - 1, 0)).astype(BF16)
        dst[f, r, :, 0:chans] = lo
        dst[f, r, :, chans : 2 * chans] = value
        dst[f, r, :, 2 * chans : 3 * chans] = hi

    local[0].wait()

    @pl.loop(0, frames * height)
    def _(n):
        f, r = n // height, lax.rem(n, height)
        value = xc[f, r]
        spread(value, xs, f, r + 1)
        xt[f, r + 1] = value.T

    local[1].wait()

    def settle(hidden, f, r, rows):
        square = hidden * hidden
        t = jnp.tanh(ROOT * hidden * (1.0 + CUBE * square))
        half = 0.5 * (1.0 + t)
        act = (hidden * half).astype(BF16)
        slope = half + (0.5 * ROOT) * hidden * (1.0 - t * t) * (1.0 + (3.0 * CUBE) * square)
        deriv[f, pl.ds(r, rows)] = slope.reshape(rows, wide, chans)
        abuf[2 + f, pl.ds(r, rows)] = act.reshape(rows, wide, chans)
        for n in range(rows):
            at[f, r + n] = act[n * wide : (n + 1) * wide].T

    def taps(src, f, r, rows):
        return jnp.concatenate(
            [src[f, pl.ds(r + i, rows)].reshape(rows * wide, 3 * chans) for i in range(3)], axis=1
        )

    @pl.loop(0, frames)
    def _(f):
        settle(dot(taps(xs, f, 1, height - 2), w[...]), f, 1, height - 2)

    for n in range(9):
        wback[(8 - n) * chans : (9 - n) * chans] = w[n * chans : (n + 1) * chans].T
    local[2].wait()
    for n in range(5):
        wtback[(4 - n) * chans : (5 - n) * chans] = wt[n * chans : (n + 1) * chans].T

    for copy in x_rows:
        copy.wait()

    @pl.loop(0, frames)
    def _(f):
        for side in range(2):
            value = xhalo[side, f]
            spread(value, xs, f, side * (height + 1))
            xt[f, side * (height + 1)] = value.T

    @pl.loop(0, frames)
    def _(f):
        lhs = jnp.concatenate([taps(xs, f, 0, 1), taps(xs, f, height - 1, 1)], axis=0)
        hidden = dot(lhs, w[...])
        settle(hidden[:wide], f, 0, 1)
        settle(hidden[wide:], f, height - 1, 1)

    a_frames = frame_pair(abuf, 2, abuf, 2)
    frames_start(a_frames)

    def segment(stream, k):
        start = streams[stream][0]
        for kind, axis, bit, size, _ in steps_of[stream][:k]:
            if kind == "halve":
                start = start + partner(axis, bit)[1] * size
            if kind == "group":
                start = start + chip * size
        return pl.multiple_of(start, ALIGN) if k else start

    def reduce_copies(stream, k):
        kind, axis, bit, size, offset = steps_of[stream][k]
        start = segment(stream, k)
        if kind == "group":
            moves = [
                (chip_peer(d), start + lax.rem(chip + d, chips) * size) for d in range(1, chips)
            ]
        else:
            peer, at_bit = partner(axis, bit)
            moves = [(peer, start + (1 - at_bit) * size if kind == "halve" else start)]
        out = []
        for n, (peer, source) in enumerate(moves):
            place = pl.ds(offset + n * size, size)
            out.append(
                (
                    remote(
                        sbuf.at[place], rbuf.at[place],
                        rsend.at[stream, k + n], rrecv.at[stream, k + n], peer,
                    ),
                    place,
                    pl.ds(pl.multiple_of(source, ALIGN), size),
                )
            )
        return out

    def reduce_start(stream, k):
        for copy, place, source in reduce_copies(stream, k):
            sbuf[place] = acc[source].astype(BF16)
            copy.start()

    def reduce_finish(stream, k):
        copies = reduce_copies(stream, k)
        for copy, _, _ in copies:
            copy.wait()
        kind, _, _, size, _ = steps_of[stream][k]
        keep = pl.ds(segment(stream, k + 1), size)
        total = sbuf[copies[0][1]].astype(F32) if kind == "whole" else acc[keep]
        for _, place, _ in copies:
            total = total + rbuf[place].astype(F32)
        acc[keep] = total

    def gather_copies(stream, k):
        kind, axis, bit, size, _ = steps_of[stream][k]
        place = gath.at[pl.ds(segment(stream, k + 1), size)]
        if kind == "group":
            to = [chip_peer(d) for d in range(1, chips)]
        else:
            to = [partner(axis, bit)[0]]
        return [
            remote(place, place, asend.at[stream, k + n], arecv.at[stream, k + n], peer)
            for n, peer in enumerate(to)
        ]

    def gather_start(stream, k):
        for copy in gather_copies(stream, k):
            copy.start()

    def gather_finish(stream, k):
        for copy in gather_copies(stream, k):
            copy.wait()

    def out_copies(stream):
        base, rows = streams[stream]
        edge = 5 * chans
        out = []
        for n, (lo, hi, ref) in enumerate(
            (
                (base, min(base + rows, edge), tgrad_ref),
                (max(base, edge), base + rows, sgrad_ref),
            )
        ):
            if lo < hi:
                out.append(
                    pltpu.make_async_copy(
                        gath.at[pl.ds(lo, hi - lo)],
                        ref.at[pl.ds(lo - n * edge, hi - lo)],
                        osem.at[2 * stream + n],
                    )
                )
        return out

    def states(stream):
        count = len(steps_of[stream])
        back = [k for k in range(count) if steps_of[stream][k][0] != "whole"][::-1]
        moves = [lambda: reduce_start(stream, 0)]
        for k in range(1, count):
            def move(k=k):
                reduce_finish(stream, k - 1)
                reduce_start(stream, k)
            moves.append(move)

        def turn():
            reduce_finish(stream, count - 1)
            place = pl.ds(segment(stream, count), steps_of[stream][-1][3])
            gath[place] = acc[place].astype(BF16)
            gather_start(stream, back[0])

        moves.append(turn)
        for last, now in zip(back, back[1:]):
            def move(last=last, now=now):
                gather_finish(stream, last)
                gather_start(stream, now)
            moves.append(move)

        def close():
            gather_finish(stream, back[-1])
            for copy in out_copies(stream):
                copy.start()

        moves.append(close)
        return moves

    queues = [states(s) for s in range(len(streams))]

    def advance(*which):
        for s in which:
            if queues[s]:
                queues[s].pop(0)()

    def act_by_grad(k, first, last):
        lhs = jnp.concatenate([at[u, r] for u in range(first, last) for r in range(height)], axis=1)
        rhs = gbuf[4 - k + first : 4 - k + last]
        return dot(lhs, rhs.reshape((last - first) * height * wide, chans))

    local[3].wait()
    own = [(max(0, k - 2), min(frames, frames + k - 2)) for k in range(5)]
    for k, (first, last) in enumerate(own):
        if first < last:
            acc[k * chans : (k + 1) * chans] = act_by_grad(k, first, last)
    frames_wait(g_frames)
    for k, (first, last) in enumerate(own):
        rows = slice(k * chans, (k + 1) * chans)
        if first >= last:
            acc[rows] = act_by_grad(k, 0, frames)
        elif first > 0:
            acc[rows] += act_by_grad(k, 0, first)
        elif last < frames:
            acc[rows] += act_by_grad(k, last, frames)
        if k % 2:
            advance(k // 2)

    def over_frames(buf, f, weight):
        lhs = jnp.concatenate(
            [buf[f + k].reshape(height * wide, chans) for k in range(5)], axis=1
        )
        return dot(lhs, weight[...])

    @pl.loop(0, frames)
    def _(f):
        act_grad = over_frames(gbuf, f, wtback).astype(BF16).astype(F32)
        hg = act_grad * deriv[f].reshape(height * wide, chans)
        hgc[f] = hg.astype(BF16).reshape(height, wide, chans)

    h_rows = row_pair(hgc, hghalo, hsend, hrecv, 2)
    for copy in h_rows:
        copy.start()
    advance(0, 1)

    @pl.loop(0, frames * height)
    def _(n):
        f, r = n // height, lax.rem(n, height)
        spread(hgc[f, r], hgs, f, r + 1)

    ready = [(2, 3), (4,), (5, 6)]
    for i in range(3):
        lhs = jnp.concatenate(
            [xt[f, r + i] for f in range(frames) for r in range(height)], axis=1
        )
        rhs = hgs[:, 1 : height + 1].reshape(frames * height * wide, 3 * chans)
        out = dot(lhs, rhs)
        for j in range(3):
            first = (5 + 3 * i + j) * chans
            acc[first : first + chans] = out[:, (2 - j) * chans : (3 - j) * chans]
        advance(*ready[i])
        if i:
            advance(0, 1)
        if i == 2:
            advance(2, 3, 4)

    for copy in h_rows:
        copy.wait()

    @pl.loop(0, frames)
    def _(f):
        for side in range(2):
            spread(hghalo[side, f], hgs, f, side * (height + 1))

    def round_of_moves():
        advance(*range(len(queues)))

    done = []

    def put(slot, value, out, f, r, rows):
        stage[slot, f, r : r + rows] = value.astype(BF16).reshape(rows, wide, chans)
        copy = pltpu.make_async_copy(
            stage.at[slot, f, pl.ds(r, rows)],
            out.at[f, pl.ds(r, rows)],
            osem.at[2 * len(queues) + len(done)],
        )
        copy.start()
        done.append(copy)

    part = height // 2
    round_of_moves()
    for f in range(frames):
        for r in range(0, height, part):
            put(0, dot(taps(hgs, f, r, part), wback[...]), fg_ref, f, r, part)
            round_of_moves()

    frames_wait(a_frames)
    for f in range(frames):
        put(1, over_frames(abuf, f, wt), block_ref, f, 0, height)
        round_of_moves()
    while any(queues):
        round_of_moves()
    for stream in range(len(queues)):
        done.extend(out_copies(stream))
    for copy in done:
        copy.wait()


def shards(sizes, fields, out_grad, spatial_weight, temporal_weight):
    samples, frames, height, wide, chans = fields.shape
    ntaps, ktaps = 9, temporal_weight.shape[0]
    unit = 2 * chans
    streams = [(n * unit, unit) for n in range((ntaps + ktaps) // 2)]
    chips = sizes["tm"] // 2
    core = [("tm", 0)]
    space = [("space", b) for b in bits_of(sizes["space"])]
    samp = [("samples", b) for b in bits_of(sizes["samples"])]
    orders = [core + (space + samp if n % 2 else samp + space) for n in range(len(streams))]
    steps_of, buffer_rows = plan(streams, orders, ("tm", 1, chips))
    most = max(len(steps) for steps in steps_of) + chips - 1
    rows_all = (ntaps + ktaps) * chans
    tile = (height, wide, chans)
    sem = pltpu.SemaphoreType.DMA
    any_spec = pl.BlockSpec(memory_space=pl.ANY)
    block, fg, sgrad, tgrad = pl.pallas_call(
        functools.partial(kernel, sizes, streams, steps_of, chips),
        out_shape=(
            jax.ShapeDtypeStruct((samples * frames,) + tile, BF16),
            jax.ShapeDtypeStruct((samples * frames,) + tile, BF16),
            jax.ShapeDtypeStruct((ntaps * chans, chans), BF16),
            jax.ShapeDtypeStruct((ktaps * chans, chans), BF16),
        ),
        in_specs=[any_spec] * 4,
        out_specs=(any_spec,) * 4,
        scratch_shapes=[
            pltpu.VMEM((frames,) + tile, BF16),
            pltpu.VMEM((frames, height + 2, wide, 3 * chans), BF16),
            pltpu.VMEM((frames, height + 2, chans, wide), BF16),
            pltpu.VMEM((2, frames, wide, chans), BF16),
            pltpu.VMEM((frames + 4,) + tile, BF16),
            pltpu.VMEM((frames + 4,) + tile, BF16),
            pltpu.VMEM((frames, height, chans, wide), BF16),
            pltpu.VMEM((frames,) + tile, F32),
            pltpu.VMEM((frames,) + tile, BF16),
            pltpu.VMEM((frames, height + 2, wide, 3 * chans), BF16),
            pltpu.VMEM((2, frames, wide, chans), BF16),
            pltpu.VMEM((ntaps * chans, chans), BF16),
            pltpu.VMEM((ntaps * chans, chans), BF16),
            pltpu.VMEM((ktaps * chans, chans), BF16),
            pltpu.VMEM((ktaps * chans, chans), BF16),
            pltpu.VMEM((rows_all, chans), F32),
            pltpu.VMEM((rows_all, chans), BF16),
            pltpu.VMEM((buffer_rows, chans), BF16),
            pltpu.VMEM((buffer_rows, chans), BF16),
            pltpu.VMEM((2, frames) + tile, BF16),
            sem((4,)), sem((2 * len(streams) + 3 * frames,)),
            sem((4,)), sem((4,)), sem((4,)), sem((4,)),
            sem((len(streams), most)), sem((len(streams), most)),
            sem((len(streams), most)), sem((len(streams), most)),
        ],
        compiler_params=pltpu.CompilerParams(
            collective_id=0, has_side_effects=True, vmem_limit_bytes=60 * 1024 * 1024
        ),
    )(
        fields.reshape((samples * frames,) + tile),
        out_grad.reshape((samples * frames,) + tile),
        spatial_weight.reshape(ntaps * chans, chans),
        temporal_weight.reshape(ktaps * chans, chans),
    )
    devices = sizes["tm"] * sizes["space"] * sizes["samples"]
    factor = (samples * frames * height * wide * devices) ** (-0.5)
    return (
        block.reshape(fields.shape),
        fg.reshape(fields.shape),
        sgrad.astype(F32).reshape(spatial_weight.shape) * factor,
        tgrad.astype(F32).reshape(temporal_weight.shape) * factor,
    )


def solution(mesh):
    split = P("samples", "tm", "space", None, None)
    return jax.shard_map(
        functools.partial(shards, dict(mesh.shape)),
        mesh=mesh,
        in_specs=(split, split, P(), P()),
        out_specs=(split, split, P(), P()),
        check_vma=False,
    )
```

```python
import functools

import jax
import jax.numpy as jnp
from jax import lax
from jax.experimental import pallas as pl
from jax.experimental.pallas import tpu as pltpu
from jax.sharding import PartitionSpec as P

F32 = jnp.float32
BF16 = jnp.bfloat16
MESH = pl.DeviceIdType.MESH
ROOT = 0.7978845608028654
CUBE = 0.044715
ALIGN = 16


def dot(a, b):
    return jnp.dot(a, b, preferred_element_type=F32)


def bits_of(size):
    return [b for b in range(size.bit_length()) if (1 << b) < size]


def plan(streams, orders, group):
    offset, steps_of = 0, []
    for (_, rows), order in zip(streams, orders):
        steps, now = [], rows
        for axis, bit in order:
            halve = now % (2 * ALIGN) == 0
            now = now // 2 if halve else now
            steps.append(("halve" if halve else "whole", axis, bit, now, offset))
            offset += now
        axis, shift, size = group
        if size > 1 and now % (size * ALIGN) == 0:
            now //= size
            steps.append(("group", axis, shift, now, offset))
            offset += now * (size - 1)
        elif size > 1:
            for bit in bits_of(size):
                steps.append(("whole", axis, bit + shift, now, offset))
                offset += now
        steps_of.append(steps)
    return steps_of, offset


def kernel(
    sizes, streams, steps_of, chips,
    x_hbm, g_hbm, w_hbm, wt_hbm,
    block_ref, fg_ref, sgrad_ref, tgrad_ref,
    xc, xs, xt, xhalo, gbuf, abuf, at, deriv, hgc, hgs, hghalo,
    w, wback, wt, wtback, acc, gath, sbuf, rbuf,
    stage, lsem, osem, hsend, hrecv, fsend, frecv, rsend, rrecv, asend, arecv,
):
    frames, height, wide, chans = xc.shape
    me, sp = lax.axis_index("tm"), lax.axis_index("space")
    here = {name: lax.axis_index(name) for name in sizes}
    has_prev, has_next = me > 0, me < sizes["tm"] - 1
    below = {"tm": lax.rem(me + sizes["tm"] - 1, sizes["tm"])}
    above = {"tm": lax.rem(me + 1, sizes["tm"])}
    left = {"space": lax.rem(sp + sizes["space"] - 1, sizes["space"])}
    right = {"space": lax.rem(sp + 1, sizes["space"])}

    def partner(axis, bit):
        at_bit = lax.rem(here[axis] // (1 << bit), 2)
        return {axis: here[axis] + (1 - 2 * at_bit) * (1 << bit)}, at_bit

    local = [
        pltpu.make_async_copy(src, dst, lsem.at[n])
        for n, (src, dst) in enumerate(
            ((x_hbm, xc), (w_hbm, w), (wt_hbm, wt), (g_hbm, gbuf.at[pl.ds(2, frames)]))
        )
    ]
    for copy in local:
        copy.start()

    chip, core = here["tm"] // 2, lax.rem(here["tm"], 2)

    def chip_peer(step):
        return {"tm": lax.rem(chip + step + chips, chips) * 2 + core}

    barrier = pltpu.get_barrier_semaphore()
    peers = [left, right, partner("tm", 0)[0]] + [chip_peer(d) for d in range(1, chips)]
    peers += [partner(a, b)[0] for a in ("space", "samples") for b in bits_of(sizes[a])]
    for peer in peers:
        pl.semaphore_signal(barrier, inc=1, device_id=peer, device_id_type=MESH)

    @pl.when(has_prev)
    def _():
        pl.semaphore_signal(barrier, inc=1, device_id=below, device_id_type=MESH)

    @pl.when(has_next)
    def _():
        pl.semaphore_signal(barrier, inc=1, device_id=above, device_id_type=MESH)

    pl.semaphore_wait(
        barrier, len(peers) + jnp.minimum(me, 1) + jnp.minimum(sizes["tm"] - 1 - me, 1)
    )

    def remote(src, dst, send, recv, peer):
        return pltpu.make_async_remote_copy(
            src_ref=src, dst_ref=dst, send_sem=send, recv_sem=recv,
            device_id=peer, device_id_type=MESH,
        )

    def row_pair(src, halo, send, recv, first):
        return [
            remote(src.at[:, height - 1], halo.at[0], send.at[first], recv.at[first], right),
            remote(src.at[:, 0], halo.at[1], send.at[first + 1], recv.at[first + 1], left),
        ]

    def frame_pair(src, start, buf, first):
        return (
            remote(
                src.at[pl.ds(start + frames - 2, 2)], buf.at[pl.ds(0, 2)],
                fsend.at[first], frecv.at[first], above,
            ),
            remote(
                src.at[pl.ds(start, 2)], buf.at[pl.ds(2 + frames, 2)],
                fsend.at[first + 1], frecv.at[first + 1], below,
            ),
        )

    def frames_start(pair):
        @pl.when(has_next)
        def _():
            pair[0].start()

        @pl.when(has_prev)
        def _():
            pair[1].start()

    def frames_wait(pair):
        @pl.when(has_next)
        def _():
            pair[0].wait_send()
            pair[1].wait_recv()

        @pl.when(has_prev)
        def _():
            pair[1].wait_send()
            pair[0].wait_recv()

    x_rows = row_pair(x_hbm, xhalo, hsend, hrecv, 0)
    g_frames = frame_pair(g_hbm, 0, gbuf, 0)
    frames_start(g_frames)
    for copy in x_rows:
        copy.start()

    for buf in (gbuf, abuf):
        @pl.when(jnp.logical_not(has_prev))
        def _(buf=buf):
            buf[0:2] = jnp.zeros((2, height, wide, chans), BF16)

        @pl.when(jnp.logical_not(has_next))
        def _(buf=buf):
            buf[2 + frames :] = jnp.zeros((2, height, wide, chans), BF16)

    cell = lax.broadcasted_iota(jnp.int32, (wide, chans), 0)

    def spread(value, dst, f, r):
        full = value.astype(F32)
        lo = jnp.where(cell == 0, 0.0, pltpu.roll(full, 1, 0)).astype(BF16)
        hi = jnp.where(cell == wide - 1, 0.0, pltpu.roll(full, wide - 1, 0)).astype(BF16)
        dst[f, r, :, 0:chans] = lo
        dst[f, r, :, chans : 2 * chans] = value
        dst[f, r, :, 2 * chans : 3 * chans] = hi

    local[0].wait()

    @pl.loop(0, frames * height)
    def _(n):
        f, r = n // height, lax.rem(n, height)
        value = xc[f, r]
        spread(value, xs, f, r + 1)
        xt[f, r + 1] = value.T

    local[1].wait()

    def settle(hidden, f, r, rows):
        square = hidden * hidden
        t = jnp.tanh(ROOT * hidden * (1.0 + CUBE * square))
        half = 0.5 * (1.0 + t)
        act = (hidden * half).astype(BF16)
        slope = half + (0.5 * ROOT) * hidden * (1.0 - t * t) * (1.0 + (3.0 * CUBE) * square)
        deriv[f, pl.ds(r, rows)] = slope.reshape(rows, wide, chans)
        abuf[2 + f, pl.ds(r, rows)] = act.reshape(rows, wide, chans)
        for n in range(rows):
            at[f, r + n] = act[n * wide : (n + 1) * wide].T

    def taps(src, f, r, rows):
        return jnp.concatenate(
            [src[f, pl.ds(r + i, rows)].reshape(rows * wide, 3 * chans) for i in range(3)], axis=1
        )

    @pl.loop(0, frames)
    def _(f):
        settle(dot(taps(xs, f, 1, height - 2), w[...]), f, 1, height - 2)

    for n in range(9):
        wback[(8 - n) * chans : (9 - n) * chans] = w[n * chans : (n + 1) * chans].T
    local[2].wait()
    for n in range(5):
        wtback[(4 - n) * chans : (5 - n) * chans] = wt[n * chans : (n + 1) * chans].T

    for copy in x_rows:
        copy.wait()

    @pl.loop(0, frames)
    def _(f):
        for side in range(2):
            value = xhalo[side, f]
            spread(value, xs, f, side * (height + 1))
            xt[f, side * (height + 1)] = value.T

    @pl.loop(0, frames)
    def _(f):
        lhs = jnp.concatenate([taps(xs, f, 0, 1), taps(xs, f, height - 1, 1)], axis=0)
        hidden = dot(lhs, w[...])
        settle(hidden[:wide], f, 0, 1)
        settle(hidden[wide:], f, height - 1, 1)

    a_frames = frame_pair(abuf, 2, abuf, 2)
    frames_start(a_frames)

    def segment(stream, k):
        start = streams[stream][0]
        for kind, axis, bit, size, _ in steps_of[stream][:k]:
            if kind == "halve":
                start = start + partner(axis, bit)[1] * size
            if kind == "group":
                start = start + chip * size
        return pl.multiple_of(start, ALIGN) if k else start

    def reduce_copies(stream, k):
        kind, axis, bit, size, offset = steps_of[stream][k]
        start = segment(stream, k)
        if kind == "group":
            moves = [
                (chip_peer(d), start + lax.rem(chip + d, chips) * size) for d in range(1, chips)
            ]
        else:
            peer, at_bit = partner(axis, bit)
            moves = [(peer, start + (1 - at_bit) * size if kind == "halve" else start)]
        out = []
        for n, (peer, source) in enumerate(moves):
            place = pl.ds(offset + n * size, size)
            out.append(
                (
                    remote(
                        sbuf.at[place], rbuf.at[place],
                        rsend.at[stream, k + n], rrecv.at[stream, k + n], peer,
                    ),
                    place,
                    pl.ds(pl.multiple_of(source, ALIGN), size),
                )
            )
        return out

    def reduce_start(stream, k):
        for copy, place, source in reduce_copies(stream, k):
            sbuf[place] = acc[source].astype(BF16)
            copy.start()

    def reduce_finish(stream, k):
        copies = reduce_copies(stream, k)
        for copy, _, _ in copies:
            copy.wait()
        kind, _, _, size, _ = steps_of[stream][k]
        keep = pl.ds(segment(stream, k + 1), size)
        total = sbuf[copies[0][1]].astype(F32) if kind == "whole" else acc[keep]
        for _, place, _ in copies:
            total = total + rbuf[place].astype(F32)
        acc[keep] = total

    def gather_copies(stream, k):
        kind, axis, bit, size, _ = steps_of[stream][k]
        place = gath.at[pl.ds(segment(stream, k + 1), size)]
        if kind == "group":
            to = [chip_peer(d) for d in range(1, chips)]
        else:
            to = [partner(axis, bit)[0]]
        return [
            remote(place, place, asend.at[stream, k + n], arecv.at[stream, k + n], peer)
            for n, peer in enumerate(to)
        ]

    def gather_start(stream, k):
        for copy in gather_copies(stream, k):
            copy.start()

    def gather_finish(stream, k):
        for copy in gather_copies(stream, k):
            copy.wait()

    def out_copies(stream):
        base, rows = streams[stream]
        edge = 5 * chans
        out = []
        for n, (lo, hi, ref) in enumerate(
            (
                (base, min(base + rows, edge), tgrad_ref),
                (max(base, edge), base + rows, sgrad_ref),
            )
        ):
            if lo < hi:
                out.append(
                    pltpu.make_async_copy(
                        gath.at[pl.ds(lo, hi - lo)],
                        ref.at[pl.ds(lo - n * edge, hi - lo)],
                        osem.at[2 * stream + n],
                    )
                )
        return out

    def states(stream):
        count = len(steps_of[stream])
        back = [k for k in range(count) if steps_of[stream][k][0] != "whole"][::-1]
        moves = [lambda: reduce_start(stream, 0)]
        for k in range(1, count):
            def move(k=k):
                reduce_finish(stream, k - 1)
                reduce_start(stream, k)
            moves.append(move)

        def turn():
            reduce_finish(stream, count - 1)
            place = pl.ds(segment(stream, count), steps_of[stream][-1][3])
            gath[place] = acc[place].astype(BF16)
            gather_start(stream, back[0])

        moves.append(turn)
        for last, now in zip(back, back[1:]):
            def move(last=last, now=now):
                gather_finish(stream, last)
                gather_start(stream, now)
            moves.append(move)

        def close():
            gather_finish(stream, back[-1])
            for copy in out_copies(stream):
                copy.start()

        moves.append(close)
        return moves

    queues = [states(s) for s in range(len(streams))]

    def advance(*which):
        for s in which:
            if queues[s]:
                queues[s].pop(0)()

    def act_by_grad(k, first, last):
        lhs = jnp.concatenate([at[u, r] for u in range(first, last) for r in range(height)], axis=1)
        rhs = gbuf[4 - k + first : 4 - k + last]
        return dot(lhs, rhs.reshape((last - first) * height * wide, chans))

    local[3].wait()
    own = [(max(0, k - 2), min(frames, frames + k - 2)) for k in range(5)]
    for k, (first, last) in enumerate(own):
        if first < last:
            acc[k * chans : (k + 1) * chans] = act_by_grad(k, first, last)
    frames_wait(g_frames)
    for k, (first, last) in enumerate(own):
        rows = slice(k * chans, (k + 1) * chans)
        if first >= last:
            acc[rows] = act_by_grad(k, 0, frames)
        elif first > 0:
            acc[rows] += act_by_grad(k, 0, first)
        elif last < frames:
            acc[rows] += act_by_grad(k, last, frames)
        if k % 2:
            advance(k // 2)

    def over_frames(buf, f, weight):
        lhs = jnp.concatenate(
            [buf[f + k].reshape(height * wide, chans) for k in range(5)], axis=1
        )
        return dot(lhs, weight[...])

    @pl.loop(0, frames)
    def _(f):
        act_grad = over_frames(gbuf, f, wtback).astype(BF16).astype(F32)
        hg = act_grad * deriv[f].reshape(height * wide, chans)
        hgc[f] = hg.astype(BF16).reshape(height, wide, chans)

    h_rows = row_pair(hgc, hghalo, hsend, hrecv, 2)
    for copy in h_rows:
        copy.start()
    advance(0, 1)

    @pl.loop(0, frames * height)
    def _(n):
        f, r = n // height, lax.rem(n, height)
        spread(hgc[f, r], hgs, f, r + 1)

    ready = [(2, 3), (4,), (5, 6)]
    for i in range(3):
        lhs = jnp.concatenate(
            [xt[f, r + i] for f in range(frames) for r in range(height)], axis=1
        )
        rhs = hgs[:, 1 : height + 1].reshape(frames * height * wide, 3 * chans)
        out = dot(lhs, rhs)
        for j in range(3):
            first = (5 + 3 * i + j) * chans
            acc[first : first + chans] = out[:, (2 - j) * chans : (3 - j) * chans]
        advance(*ready[i])
        if i:
            advance(0, 1)
        if i == 2:
            advance(2, 3, 4)

    for copy in h_rows:
        copy.wait()

    @pl.loop(0, frames)
    def _(f):
        for side in range(2):
            spread(hghalo[side, f], hgs, f, side * (height + 1))

    rounds = []

    def round_of_moves():
        advance(*range(2 if len(rounds) < 3 else 0, len(queues)))
        rounds.append(0)

    done = []

    def put(slot, value, out, f, r, rows):
        stage[slot, f, r : r + rows] = value.astype(BF16).reshape(rows, wide, chans)
        copy = pltpu.make_async_copy(
            stage.at[slot, f, pl.ds(r, rows)],
            out.at[f, pl.ds(r, rows)],
            osem.at[2 * len(queues) + len(done)],
        )
        copy.start()
        done.append(copy)

    part = height // 2
    round_of_moves()
    for f in range(frames):
        for r in range(0, height, part):
            put(0, dot(taps(hgs, f, r, part), wback[...]), fg_ref, f, r, part)
            round_of_moves()

    frames_wait(a_frames)
    for f in range(frames):
        put(1, over_frames(abuf, f, wt), block_ref, f, 0, height)
        round_of_moves()
    while any(queues):
        round_of_moves()
    for stream in range(len(queues)):
        done.extend(out_copies(stream))
    for copy in done:
        copy.wait()


def shards(sizes, fields, out_grad, spatial_weight, temporal_weight):
    samples, frames, height, wide, chans = fields.shape
    ntaps, ktaps = 9, temporal_weight.shape[0]
    unit = 2 * chans
    streams = [(n * unit, unit) for n in range((ntaps + ktaps) // 2)]
    chips = sizes["tm"] // 2
    core = [("tm", 0)]
    space = [("space", b) for b in bits_of(sizes["space"])]
    samp = [("samples", b) for b in bits_of(sizes["samples"])]
    orders = [core + (space + samp if n % 2 else samp + space) for n in range(len(streams))]
    steps_of, buffer_rows = plan(streams, orders, ("tm", 1, chips))
    most = max(len(steps) for steps in steps_of) + chips - 1
    rows_all = (ntaps + ktaps) * chans
    tile = (height, wide, chans)
    sem = pltpu.SemaphoreType.DMA
    any_spec = pl.BlockSpec(memory_space=pl.ANY)
    block, fg, sgrad, tgrad = pl.pallas_call(
        functools.partial(kernel, sizes, streams, steps_of, chips),
        out_shape=(
            jax.ShapeDtypeStruct((samples * frames,) + tile, BF16),
            jax.ShapeDtypeStruct((samples * frames,) + tile, BF16),
            jax.ShapeDtypeStruct((ntaps * chans, chans), BF16),
            jax.ShapeDtypeStruct((ktaps * chans, chans), BF16),
        ),
        in_specs=[any_spec] * 4,
        out_specs=(any_spec,) * 4,
        scratch_shapes=[
            pltpu.VMEM((frames,) + tile, BF16),
            pltpu.VMEM((frames, height + 2, wide, 3 * chans), BF16),
            pltpu.VMEM((frames, height + 2, chans, wide), BF16),
            pltpu.VMEM((2, frames, wide, chans), BF16),
            pltpu.VMEM((frames + 4,) + tile, BF16),
            pltpu.VMEM((frames + 4,) + tile, BF16),
            pltpu.VMEM((frames, height, chans, wide), BF16),
            pltpu.VMEM((frames,) + tile, F32),
            pltpu.VMEM((frames,) + tile, BF16),
            pltpu.VMEM((frames, height + 2, wide, 3 * chans), BF16),
            pltpu.VMEM((2, frames, wide, chans), BF16),
            pltpu.VMEM((ntaps * chans, chans), BF16),
            pltpu.VMEM((ntaps * chans, chans), BF16),
            pltpu.VMEM((ktaps * chans, chans), BF16),
            pltpu.VMEM((ktaps * chans, chans), BF16),
            pltpu.VMEM((rows_all, chans), F32),
            pltpu.VMEM((rows_all, chans), BF16),
            pltpu.VMEM((buffer_rows, chans), BF16),
            pltpu.VMEM((buffer_rows, chans), BF16),
            pltpu.VMEM((2, frames) + tile, BF16),
            sem((4,)), sem((2 * len(streams) + 3 * frames,)),
            sem((4,)), sem((4,)), sem((4,)), sem((4,)),
            sem((len(streams), most)), sem((len(streams), most)),
            sem((len(streams), most)), sem((len(streams), most)),
        ],
        compiler_params=pltpu.CompilerParams(
            collective_id=0, has_side_effects=True, vmem_limit_bytes=60 * 1024 * 1024
        ),
    )(
        fields.reshape((samples * frames,) + tile),
        out_grad.reshape((samples * frames,) + tile),
        spatial_weight.reshape(ntaps * chans, chans),
        temporal_weight.reshape(ktaps * chans, chans),
    )
    devices = sizes["tm"] * sizes["space"] * sizes["samples"]
    factor = (samples * frames * height * wide * devices) ** (-0.5)
    return (
        block.reshape(fields.shape),
        fg.reshape(fields.shape),
        sgrad.astype(F32).reshape(spatial_weight.shape) * factor,
        tgrad.astype(F32).reshape(temporal_weight.shape) * factor,
    )


def solution(mesh):
    split = P("samples", "tm", "space", None, None)
    return jax.shard_map(
        functools.partial(shards, dict(mesh.shape)),
        mesh=mesh,
        in_specs=(split, split, P(), P()),
        out_specs=(split, split, P(), P()),
        check_vma=False,
    )
```
